768 devices in a mesh: dp: 8 (over y), row: 8 (over z_lo, core), col: 12 (over x, z_hi).
Axes of the slice: x: 4, y: 8, z: 12 (z_hi: 3, z_lo: 4; z = z_hi * 4 + z_lo), core: 2. Of those that a mesh axis runs over, the one named last changes fastest.
Arguments:
- inputs: bfloat16 [12288, 6144], P('dp', 'row'), may hold values from -6 to 6
- pre_act: bfloat16 [12288, 12288], P(('dp', 'row'), 'col'), may hold values from -8 to 8
- out_grad: bfloat16 [12288, 12288], P(('dp', 'row'), 'col'), may hold values from -6 to 6
- weight: bfloat16 [6144, 12288], P('row', 'col'), may hold values from -6 to 6
- swag_mean: float32 [8, 768, 12288], P('dp', 'row', 'col'), may hold values from -6 to 6
- swag_square: float32 [8, 768, 12288], P('dp', 'row', 'col'), may hold values from 0.5 to 3
- snapshots: int32 [1], replicated, may hold values from 1 to 32
- update_flag: int32 [8, 768], P('dp', 'row'), may hold values 0 or 1
Outputs:
- input_grad: bfloat16 [12288, 6144], P(('dp', 'col'), 'row')
- new_weight: float32 [8, 768, 12288], P('dp', 'row', 'col')
- mean_out: float32 [8, 768, 12288], P('dp', 'row', 'col')
- square_out: float32 [8, 768, 12288], P('dp', 'row', 'col')
The draws below stay inside these ranges and needn't reach their ends.
All inputs are finite; a program needn't handle non-finite values. No bound on the sum of `update_flag` on one device may be relied on, other than what follows from the above.
Results may differ from the reference program's by a relative error of at most 0.013.
Values may be sent and summed in bfloat16 or wider, within the bound.
A program may use at most 64 MiB of HBM per device.

```python
import jax
import jax.numpy as jnp
from jax import lax

D = 6144
FF = 12288
TOK = 1536
TOKENS = 12288
SHARE = 96
N_DP = 8
N_ROW = 8
N_COL = 12


def place_ends(result, rng, smallest, largest):
    place = [jax.random.randint(jax.random.fold_in(rng, axis), (), 0, length) for axis, length in enumerate(result.shape)]
    widest = result.shape.index(max(result.shape))
    next_to = place[:widest] + [(place[widest] + 1) % result.shape[widest]] + place[widest + 1:]
    return result.at[tuple(place)].set(smallest).at[tuple(next_to)].set(largest)


def block_levels(rng, extent, split, smallest, high):
    loudness = 1.0
    for position, shards_of in split:
        heights = jax.random.uniform(jax.random.fold_in(jax.random.fold_in(rng, 6), position), (shards_of,), jnp.float32, smallest / len(split), high / len(split))
        loudness = loudness * jnp.repeat(jnp.exp(heights), extent[position] // shards_of).reshape((-1,) + (1,) * (len(extent) - 1 - position))
    return loudness


def normal_values(rng, dims, deviation, most, cuts=(), held_as=jnp.bfloat16):
    result = jax.random.normal(rng, dims, jnp.float32) * deviation
    if len(cuts) > 0:
        result = block_levels(rng, dims, cuts, -0.22, 0.18) * result
    return jnp.clip(result, min=-most, max=most).astype(held_as)


def setup_inputs(seed: int = 0) -> dict:
    keys = jax.random.split(jax.random.key(seed), 9)
    inputs = normal_values(keys[0], (TOKENS, D), 1.0, 6.0, ((0, 8), (1, 8)))
    pre_act = normal_values(keys[1], (TOKENS, FF), 1.5, 8.0, ((0, 64), (1, 12)))
    out_grad = normal_values(keys[2], (TOKENS, FF), 1.0, 6.0, ((0, 64), (1, 12)))
    weight = normal_values(keys[3], (D, FF), 1.0, 6.0, ((0, 8), (1, 12)))
    swag_mean = normal_values(keys[4], (N_DP, D // N_DP, FF), 1.0, 6.0, ((0, 8), (1, 8), (2, 12)), jnp.float32)
    swag_square = jnp.clip(0.5 + 2.5 * jax.random.uniform(keys[5], (N_DP, D // N_DP, FF), jnp.float32) ** block_levels(keys[5], (N_DP, D // N_DP, FF), ((0, 8), (1, 8), (2, 12)), -0.2, 0.2), 0.5, 3.0)
    snapshots = jax.random.randint(keys[6], (1,), 1, 33).astype(jnp.int32)
    update_flag = place_ends((jax.random.randint(keys[7], (N_DP, D // N_DP), 0, 2) < 1).astype(jnp.int32), jax.random.fold_in(keys[7], 1), 0, 1)
    return dict(inputs=inputs, pre_act=pre_act, out_grad=out_grad, weight=weight, swag_mean=swag_mean, swag_square=swag_square, snapshots=snapshots, update_flag=update_flag)


learning_rate = 0.5


def gelu_slope(values):
    normal_cdf = 0.5 * (1.0 + lax.erf(values * 0.7071067811865476))
    density = jnp.exp(-0.5 * values * values) * 0.3989422804014327
    return normal_cdf + values * density


def rounded(values):
    return lax.optimization_barrier(values.astype(jnp.bfloat16)).astype(jnp.float32)


def reference(inputs, pre_act, out_grad, weight, swag_mean, swag_square, snapshots, update_flag):
    multiplier = 1.0 / (D ** 0.5)
    pre_grad = (out_grad.astype(jnp.float32) * gelu_slope(pre_act.astype(jnp.float32))).astype(jnp.bfloat16)
    block_cols = FF // N_COL
    total = jnp.zeros((TOKENS, D), jnp.float32)
    for block in range(N_COL):
        grad_block = pre_grad[:, block * block_cols:(block + 1) * block_cols]
        weight_block = weight[:, block * block_cols:(block + 1) * block_cols]
        product = lax.dot_general(grad_block, weight_block, (((1,), (1,)), ((), ())), preferred_element_type=jnp.float32)
        total = total + rounded(product * multiplier)
    input_grad = total.astype(jnp.bfloat16)
    summed = jnp.zeros((D, FF), jnp.float32)
    for replica in range(N_DP):
        input_rows = inputs[replica * TOK:(replica + 1) * TOK]
        grad_rows = pre_grad[replica * TOK:(replica + 1) * TOK]
        product = lax.dot_general(input_rows, grad_rows, (((0,), (0,)), ((), ())), preferred_element_type=jnp.float32)
        summed = summed + rounded(product)
    stepped = weight.astype(jnp.float32) - learning_rate * (summed / (TOKENS ** 0.5))
    regrouped = stepped.reshape(N_ROW, N_DP, SHARE, FF).transpose(1, 0, 2, 3).reshape(N_DP, D // N_DP, FF)
    blend = update_flag.astype(jnp.float32)[:, :, None] / (snapshots[0].astype(jnp.float32) + 1.0)
    mean_out = swag_mean + blend * (regrouped - swag_mean)
    square_out = swag_square + blend * (regrouped * regrouped - swag_square)
    return input_grad, regrouped, mean_out, square_out
```

```python
import jax
import jax.numpy as jnp
from jax import lax
from jax.experimental import pallas as pl
from jax.experimental.pallas import tpu as pltpu
from jax.sharding import PartitionSpec as P

MESH = pl.DeviceIdType.MESH
D = 6144
learning_rate = 0.5
NZ = 4
NH = 3
NK = 2
STEPS = 7


def gelu_slope(values):
    normal_cdf = 0.5 * (1.0 + lax.erf(values * 0.7071067811865476))
    density = jnp.exp(-0.5 * values * values) * 0.3989422804014327
    return normal_cdf + values * density


def remote(src, dst, send_sem, recv_sem, device):
    return pltpu.make_async_remote_copy(
        src_ref=src, dst_ref=dst, send_sem=send_sem, recv_sem=recv_sem, device_id=device, device_id_type=MESH
    )


def kernel(
    inputs_hbm, pre_hbm, out_hbm, weight_hbm, share_ref, igrad_ref,
    inp, pre, outg, wgt, portion, acc, term, opp, xrecv, zsum, zrecv, ysend, yrecv,
    load_sem, zs, zr, cs, cr, opps, oppr, xs, xr, hs, hr, ys, yr,
):
    groups = lax.axis_size("dp")
    y = lax.axis_index("dp")
    row = lax.axis_index("row")
    col = lax.axis_index("col")
    zl, c = row // 2, row % 2
    x, zh = col // NH, col % NH
    multiplier = 1.0 / D**0.5
    token_block = pre.shape[0]
    half = token_block
    piece = token_block // NK
    shard = acc.shape[0] // groups
    cols = acc.shape[1] // 2

    partner = {"row": row + 1 - 2 * c}
    z_up, z_down = {"row": row + 2}, {"row": row - 2}
    x_up = {"col": (x + 1) % NZ * NH + zh}
    x_down = {"col": (x + NZ - 1) % NZ * NH + zh}
    h_peer = [{"col": x * NH + (zh + j) % NH} for j in (1, 2)]
    y_peer = [{"dp": (y + 1) % groups}, {"dp": (y + groups - 1) % groups}]

    barrier = pltpu.get_barrier_semaphore()
    greet = [
        partner, {"row": (row + 2) % (2 * NZ)}, {"row": (row + 2 * NZ - 2) % (2 * NZ)},
        x_up, x_down, *h_peer, *y_peer,
    ]
    for device in greet:
        pl.semaphore_signal(barrier, inc=1, device_id=device, device_id_type=MESH)

    loads = [
        pltpu.make_async_copy(pre_hbm, pre, load_sem.at[0]),
        pltpu.make_async_copy(out_hbm, outg, load_sem.at[1]),
        pltpu.make_async_copy(weight_hbm, wgt, load_sem.at[2]),
        pltpu.make_async_copy(inputs_hbm, inp, load_sem.at[3]),
    ]
    for load in loads:
        load.start()
    loads[0].wait()
    loads[1].wait()

    def z_copy(way, q, k):
        block = portion.at[q, c, k]
        return remote(block, block, zs.at[way, q, k], zr.at[q, k], z_up if way == 0 else z_down)

    def c_copy(q, k):
        block = portion.at[q, c, k]
        return remote(block, block, cs.at[q, k], cr.at[q, k], partner)

    def c_arrival(q, k):
        block = portion.at[q, 1 - c, k]
        return remote(block, block, cs.at[q, k], cr.at[q, k], partner)

    tile = 16

    def local_grad(k):
        def body(i, carry):
            start = pl.multiple_of(i * tile, tile)
            a = pre[pl.ds(pl.multiple_of(k * piece + start, tile), tile), :].astype(jnp.float32)
            g = outg[pl.ds(pl.multiple_of(k * piece + start, tile), tile), :].astype(jnp.float32)
            portion[zl, c, k, pl.ds(start, tile), :] = (g * gelu_slope(a)).astype(jnp.bfloat16)
            return carry

        lax.fori_loop(0, piece // tile, body, 0)

    for k in range(NK):
        local_grad(k)
        if k == 0:
            pl.semaphore_wait(barrier, len(greet))

        @pl.when(zl < NZ - 1)
        def _():
            z_copy(0, zl, k).start()

        @pl.when(zl > 0)
        def _():
            z_copy(1, zl, k).start()

        c_copy(zl, k).start()

    def zero(i, carry):
        acc[pl.ds(pl.multiple_of(i * 8, 8), 8), :] = jnp.zeros((8, acc.shape[1]), jnp.float32)
        return carry

    lax.fori_loop(0, acc.shape[0] // 8, zero, 0)
    loads[2].wait()
    loads[3].wait()

    def opp_copy(p, which):
        return remote(
            term.at[p, pl.ds(which * half, half)], opp.at[which], opps.at[which], oppr.at[which],
            x_down if which == 0 else x_up,
        )

    def x_copy(p, side, part):
        window = pl.ds(part * half, half)
        return remote(
            term.at[p, window], xrecv.at[side, window], xs.at[side, part], xr.at[side, part],
            x_down if side == 0 else x_up,
        )

    p_one = (x + NZ - 1) % NZ
    p_three = (x + 1) % NZ
    p_two = (x + 2) % NZ

    def absorb(p, which):
        opp_copy(p, which).wait_recv()
        base = which * half

        def body(i, carry):
            at = pl.multiple_of(base + i * 32, 32)
            own = term[p, pl.ds(at, 32), :].astype(jnp.float32)
            come = opp[which, pl.ds(pl.multiple_of(i * 32, 32), 32), :].astype(jnp.float32)
            term[p, pl.ds(at, 32), :] = (own + come).astype(jnp.bfloat16)
            return carry

        lax.fori_loop(0, half // 32, body, 0)
        x_copy(p, which, which).start()

    def h_copy(j):
        return remote(zsum.at[(zh + j) % NH], zrecv.at[j - 1], hs.at[j - 1], hr.at[j - 1], h_peer[j - 1])

    def collect():
        for side in range(2):
            for part in range(2):
                x_copy(x, side, part).wait_recv()
        for j in range(NH):

            def body(i, carry):
                at = pl.multiple_of(j * 128 + i * 32, 32)
                total = (
                    term[x, pl.ds(at, 32), :].astype(jnp.float32)
                    + xrecv[0, pl.ds(at, 32), :].astype(jnp.float32)
                    + xrecv[1, pl.ds(at, 32), :].astype(jnp.float32)
                )
                zsum[j, pl.ds(pl.multiple_of(i * 32, 32), 32), :] = total.astype(jnp.bfloat16)
                return carry

            lax.fori_loop(0, 128 // 32, body, 0)
        for j in (1, 2):
            h_copy(j).start()

    def later(d):
        @pl.when(jnp.abs(zl - p_one) == d - 1)
        def _():
            absorb(p_one, 0)

        @pl.when(jnp.abs(zl - p_three) == d - 1)
        def _():
            absorb(p_three, 1)

        @pl.when(jnp.abs(zl - x) == d - 2)
        def _():
            collect()

    def compute(q):
        for k in range(NK):
            c_arrival(q, k).wait_recv()
        tokens = portion[q].reshape(2 * token_block, portion.shape[-1])

        def product(n, carry):
            at = pl.ds(pl.multiple_of(n * 256, 256), 256)
            part = lax.dot_general(
                tokens, wgt[at, :], (((1,), (1,)), ((), ())), preferred_element_type=jnp.float32
            )
            term[q, :, at] = (part * multiplier).astype(jnp.bfloat16)
            return carry

        lax.fori_loop(0, wgt.shape[0] // 256, product, 0)

        @pl.when(p_two == q)
        def _():
            opp_copy(q, 0).start()
            opp_copy(q, 1).start()

        @pl.when(p_one == q)
        def _():
            x_copy(q, 0, 1).start()

        @pl.when(p_three == q)
        def _():
            x_copy(q, 1, 0).start()

        def outer(m, carry):
            at = pl.ds(pl.multiple_of(m * 256, 256), 256)
            acc[at, :] += lax.dot_general(
                inp[q, :, at], tokens, (((0,), (0,)), ((), ())), preferred_element_type=jnp.float32
            )
            return carry

        lax.fori_loop(0, acc.shape[0] // 256, outer, 0)

    def distance(d, carry):
        @pl.when(d > 0)
        def _():
            for k in range(NK):

                @pl.when(zl - d >= 0)
                def _():
                    q = zl - d
                    z_copy(0, q, k).wait_recv()

                    @pl.when(zl < NZ - 1)
                    def _():
                        z_copy(0, q, k).start()

                    c_copy(q, k).start()

                @pl.when(zl + d < NZ)
                def _():
                    q = zl + d
                    z_copy(1, q, k).wait_recv()

                    @pl.when(zl > 0)
                    def _():
                        z_copy(1, q, k).start()

                    c_copy(q, k).start()

        def side(j, carry):
            q = zl - d + 2 * d * j

            @pl.when((q >= 0) & (q < NZ))
            def _():
                compute(q)

            return carry

        lax.fori_loop(0, 1 + jnp.minimum(d, 1), side, 0)
        later(d)
        return carry

    lax.fori_loop(0, NZ, distance, 0)

    def y_copy(way, i):
        return remote(ysend.at[way, i], yrecv.at[way, i], ys.at[way, i], yr.at[way, i], y_peer[way])

    def y_step(i, absorbed):
        for way in range(2):
            k = groups // 2 - (i + 1) // 2
            target = (y + k) % groups if way == 0 else (y + groups - k) % groups
            which = (i + way) % 2
            rows = pl.ds(pl.multiple_of(target * shard, 8), shard)
            window = pl.ds(pl.multiple_of(which * cols, 128), cols)
            own = acc[rows, window]
            if absorbed:
                y_copy(way, i - 2).wait_recv()
                own = own + yrecv[way, i - 2].astype(jnp.float32)
            ysend[way, i] = own.astype(jnp.bfloat16)
            y_copy(way, i).start()

    y_step(0, False)
    y_step(1, False)

    def y_loop(i, carry):
        y_step(i, True)

        @pl.when(i == 4)
        def _():
            later(NZ)

        return carry

    lax.fori_loop(2, STEPS, y_loop, 0)
    later(NZ + 1)

    rows = pl.ds(pl.multiple_of(y * shard, 8), shard)
    for way in range(2):
        for i in (STEPS - 2, STEPS - 1):
            y_copy(way, i).wait_recv()
    share_ref[:, :cols] = (
        acc[rows, :cols] + yrecv[0, STEPS - 1].astype(jnp.float32) + yrecv[1, STEPS - 2].astype(jnp.float32)
    )
    share_ref[:, cols:] = (
        acc[rows, cols:] + yrecv[0, STEPS - 2].astype(jnp.float32) + yrecv[1, STEPS - 1].astype(jnp.float32)
    )
    for j in (1, 2):
        h_copy(j).wait_recv()
    igrad_ref[...] = (
        zsum[zh].astype(jnp.float32) + zrecv[0].astype(jnp.float32) + zrecv[1].astype(jnp.float32)
    )

    def drain(q, carry):
        for k in range(NK):
            c_copy(q, k).wait_send()

            @pl.when((q <= zl) & (zl < NZ - 1))
            def _():
                z_copy(0, q, k).wait_send()

            @pl.when((q >= zl) & (zl > 0))
            def _():
                z_copy(1, q, k).wait_send()

        return carry

    lax.fori_loop(0, NZ, drain, 0)
    for which in range(2):
        opp_copy(p_two, which).wait_send()
        x_copy(p_one, 0, which).wait_send()
        x_copy(p_three, 1, which).wait_send()
        h_copy(which + 1).wait_send()

    def y_drain(i, carry):
        y_copy(0, i).wait_send()
        y_copy(1, i).wait_send()
        return carry

    lax.fori_loop(0, STEPS, y_drain, 0)


def body(inputs, pre_act, out_grad, weight, swag_mean, swag_square, snapshots, update_flag):
    tokens, width = inputs.shape
    block, hidden = pre_act.shape
    groups = lax.axis_size("dp")
    shard = width // groups
    pair = 2 * block
    bf, f32 = jnp.bfloat16, jnp.float32
    dma = pltpu.SemaphoreType.DMA
    share, igrad = pl.pallas_call(
        kernel,
        out_shape=(
            jax.ShapeDtypeStruct((shard, hidden), f32),
            jax.ShapeDtypeStruct((pair // NH, width), f32),
        ),
        in_specs=[pl.BlockSpec(memory_space=pl.ANY)] * 4,
        out_specs=(pl.BlockSpec(memory_space=pltpu.VMEM), pl.BlockSpec(memory_space=pltpu.VMEM)),
        scratch_shapes=[
            pltpu.VMEM((NZ, pair, width), bf),
            pltpu.VMEM((block, hidden), bf),
            pltpu.VMEM((block, hidden), bf),
            pltpu.VMEM((width, hidden), bf),
            pltpu.VMEM((NZ, 2, NK, block // NK, hidden), bf),
            pltpu.VMEM((width, hidden), f32),
            pltpu.VMEM((NZ, pair, width), bf),
            pltpu.VMEM((2, block, width), bf),
            pltpu.VMEM((2, pair, width), bf),
            pltpu.VMEM((NH, pair // NH, width), bf),
            pltpu.VMEM((2, pair // NH, width), bf),
            pltpu.VMEM((2, STEPS, shard, hidden // 2), bf),
            pltpu.VMEM((2, STEPS, shard, hidden // 2), bf),
            dma((4,)),
            dma((2, NZ, NK)), dma((NZ, NK)), dma((NZ, NK)), dma((NZ, NK)),
            dma((2,)), dma((2,)), dma((2, 2)), dma((2, 2)), dma((2,)), dma((2,)),
            dma((2, STEPS)), dma((2, STEPS)),
        ],
        compiler_params=pltpu.CompilerParams(collective_id=0, has_side_effects=True),
    )(inputs.reshape(NZ, pair, width), pre_act, out_grad, weight)

    replica_index = lax.axis_index("dp")
    own_rows = lax.dynamic_slice_in_dim(weight, replica_index * shard, shard, 0).astype(f32)
    stepped = own_rows - learning_rate * (share / (tokens * groups) ** 0.5)
    blend = update_flag[0].astype(f32)[:, None] / (snapshots[0].astype(f32) + 1.0)
    mean_new = swag_mean[0] + blend * (stepped - swag_mean[0])
    square_new = swag_square[0] + blend * (stepped * stepped - swag_square[0])
    return (igrad.astype(bf), stepped[None], mean_new[None], square_new[None])


def solution(mesh):
    in_specs = (
        P("dp", "row"),
        P(("dp", "row"), "col"),
        P(("dp", "row"), "col"),
        P("row", "col"),
        P("dp", "row", "col"),
        P("dp", "row", "col"),
        P(),
        P("dp", "row"),
    )
    out_specs = (
        P(("dp", "col"), "row"),
        P("dp", "row", "col"),
        P("dp", "row", "col"),
        P("dp", "row", "col"),
    )
    return jax.shard_map(body, mesh=mesh, in_specs=in_specs, out_specs=out_specs, check_vma=False)
```

```python
import jax
import jax.numpy as jnp
from jax import lax
from jax.experimental import pallas as pl
from jax.experimental.pallas import tpu as pltpu
from jax.sharding import PartitionSpec as P

MESH = pl.DeviceIdType.MESH
D = 6144
learning_rate = 0.5
NZ = 4
NH = 3
NK = 2
STEPS = 7
ABSORB, COLLECT = 1, 3
HOLD = 0
TAIL = {1: 0, 3: 1, 4: 2}
REACH = NZ * (NH - 1)
PER = 6


def gelu_slope(values):
    normal_cdf = 0.5 * (1.0 + lax.erf(values * 0.7071067811865476))
    density = jnp.exp(-0.5 * values * values) * 0.3989422804014327
    return normal_cdf + values * density


def remote(src, dst, send_sem, recv_sem, device):
    return pltpu.make_async_remote_copy(
        src_ref=src, dst_ref=dst, send_sem=send_sem, recv_sem=recv_sem, device_id=device, device_id_type=MESH
    )


def send_orders():
    orders, starts, extras = [], [], []
    arriving = []
    for z in range(NZ):
        own = [(z, k) for k in range(NK)]
        first = NK if z == 0 else min(NK, 2 if z == NZ - 2 else 1)
        start, rest = own[:first], own[first:]
        order, extra = list(start), []
        for piece in arriving:
            order.append(piece)
            if rest:
                extra.append(rest[0][1])
                order.append(rest.pop(0))
            else:
                extra.append(-1)
        order += rest
        orders.append(order)
        starts.append(first)
        extras.append(extra)
        arriving = order
    return orders, starts, extras


def packed(entries, length):
    words = []
    for line in entries:
        line = list(line) + [-1] * (length - len(line))
        line = [e + 1 for e in line]
        words.append([
            sum(e << (5 * i) for i, e in enumerate(line[w : w + PER])) for w in range(0, length, PER)
        ])
    return words


def choose(words, zl):
    out = []
    for w in range(len(words[0])):
        value = jnp.int32(words[0][w])
        for v in range(1, NZ):
            value = jnp.where(zl == v, jnp.int32(words[v][w]), value)
        out.append(value)
    return out


def look(words, s):
    value = jnp.int32(0)
    for w, word in enumerate(words):
        value = jnp.where((s >= PER * w) & (s < PER * (w + 1)), word, value)
    return ((value >> (5 * ((s + PER) % PER))) & 31) - 1


def kernel(
    inputs_hbm, pre_hbm, out_hbm, weight_hbm, snap_hbm, flag_hbm, step_ref, igrad_ref, blend_ref,
    snap, flag, inp, pre, outg, wgt, portion, acc, term, opp, xrecv, zsum, zrecv, ysend, yrecv,
    load_sem, zs, zr, cs, cr, opps, oppr, xs, xr, hs, hr, ys, yr, token,
):
    groups = lax.axis_size("dp")
    y = lax.axis_index("dp")
    row = lax.axis_index("row")
    col = lax.axis_index("col")
    zl, c = row // 2, row % 2
    x, zh = col // NH, col % NH
    multiplier = 1.0 / D**0.5
    token_block = pre.shape[0]
    piece = token_block // NK
    hidden = portion.shape[-1]
    shard = acc.shape[0] // groups
    cols = acc.shape[1] // 2
    third = 2 * token_block // NH
    last = NZ * NK

    partner = {"row": row + 1 - 2 * c}
    z_up, z_down = {"row": row + 2}, {"row": row - 2}
    x_up = {"col": (x + 1) % NZ * NH + zh}
    x_down = {"col": (x + NZ - 1) % NZ * NH + zh}
    y_peer = [{"dp": (y + 1) % groups}, {"dp": (y + groups - 1) % groups}]

    barrier = pltpu.get_barrier_semaphore()
    greet = [partner, x_up, x_down, *y_peer]
    for device in greet:
        pl.semaphore_signal(barrier, inc=1, device_id=device, device_id_type=MESH)
    chain = NZ * NH - 1
    place = zh * NZ + zl
    line_up = {"row": (row + 2) % (2 * NZ), "col": (col + (zl + 1) // NZ) % (NZ * NH)}
    line_down = {"row": (row + 2 * NZ - 2) % (2 * NZ), "col": (col + NZ * NH - (NZ - zl) // NZ) % (NZ * NH)}

    @pl.when(place < chain)
    def _():
        pl.semaphore_signal(barrier, inc=1, device_id=line_up, device_id_type=MESH)

    @pl.when(place > 0)
    def _():
        pl.semaphore_signal(barrier, inc=1, device_id=line_down, device_id_type=MESH)

    arrivals = len(greet) + jnp.minimum(place, 1) + jnp.minimum(chain - place, 1)

    def hear(n):
        for way, there, onward, device in (
            (0, place - n >= 0, place < chain, line_up), (1, place + n <= chain, place > 0, line_down),
        ):

            @pl.when((n >= 2) & (n <= REACH) & there)
            def _():
                pl.semaphore_wait(token.at[way], 1)

            @pl.when((n < REACH) & there & onward)
            def _():
                pl.semaphore_signal(token.at[way], inc=1, device_id=device, device_id_type=MESH)

    loads = [
        pltpu.make_async_copy(pre_hbm, pre, load_sem.at[0]),
        pltpu.make_async_copy(out_hbm, outg, load_sem.at[1]),
        pltpu.make_async_copy(weight_hbm, wgt, load_sem.at[2]),
        pltpu.make_async_copy(snap_hbm, snap, load_sem.at[3]),
        pltpu.make_async_copy(flag_hbm, flag, load_sem.at[4]),
        *(
            pltpu.make_async_copy(inputs_hbm.at[q, h], inp.at[q, :, h], load_sem.at[5 + 2 * q + h])
            for q in range(NZ)
            for h in range(2)
        ),
    ]
    for load in loads:
        load.start()

    orders, starts, extras = send_orders()
    code = lambda line: [q * NK + k for q, k in line]
    flip = lambda line: [(NZ - 1 - q, k) for q, k in line]
    own_steps = [[(z, k) for k in range(NK)] for z in range(NZ)]
    none = [-1] * NK
    below = [code(own_steps[z]) + (code(orders[z - 1]) if z > 0 else []) for z in range(NZ)]
    above = [none + (code(flip(orders[NZ - 2 - z])) if z < NZ - 1 else []) for z in range(NZ)]
    more_up = [none + extras[z] for z in range(NZ)]
    more_down = [none + extras[NZ - 1 - z] for z in range(NZ)]
    start_up = choose([[starts[z]] for z in range(NZ)], zl)[0]
    start_down = choose([[starts[NZ - 1 - z]] for z in range(NZ)], zl)[0]
    below, above, more_up, more_down = (
        choose(packed(t, last), zl) for t in (below, above, more_up, more_down)
    )

    def z_copy(way, q, k):
        block = portion.at[q, k, c]
        return remote(block, block, zs.at[way, q, k], zr.at[q, k], z_up if way == 0 else z_down)

    def c_copy(q, k):
        block = portion.at[q, k, c]
        return remote(block, block, cs.at[q, k], cr.at[q, k], partner)

    def c_arrival(q, k):
        block = portion.at[q, k, 1 - c]
        return remote(block, block, cs.at[q, k], cr.at[q, k], partner)

    tile = 16

    def local_grad(k):
        def body(i, carry):
            start = pl.multiple_of(i * tile, tile)
            a = pre[pl.ds(pl.multiple_of(k * piece + start, tile), tile), :].astype(jnp.float32)
            g = outg[pl.ds(pl.multiple_of(k * piece + start, tile), tile), :].astype(jnp.float32)
            portion[zl, k, c, pl.ds(start, tile), :] = (g * gelu_slope(a)).astype(jnp.bfloat16)
            return carry

        lax.fori_loop(0, piece // tile, body, 0)

    loads[0].wait()
    loads[1].wait()
    for k in range(NK):
        local_grad(k)
        if k == 0:
            pl.semaphore_wait(barrier, arrivals)

        @pl.when((zl < NZ - 1) & (k < start_up))
        def _():
            z_copy(0, zl, k).start()

        @pl.when((zl > 0) & (k < start_down))
        def _():
            z_copy(1, zl, k).start()

        c_copy(zl, k).start()

    def zero(i, carry):
        acc[pl.ds(pl.multiple_of(i * 8, 8), 8), :] = jnp.zeros((8, acc.shape[1]), jnp.float32)
        return carry

    lax.fori_loop(0, acc.shape[0] // 8, zero, 0)
    for load in loads[2:]:
        load.wait()
    flags = jnp.broadcast_to(flag[...].astype(jnp.float32), (shard, shard))
    here = lax.broadcasted_iota(jnp.int32, (shard, shard), 0) == lax.broadcasted_iota(jnp.int32, (shard, shard), 1)
    column = jnp.sum(jnp.where(here, flags, 0.0), axis=1, keepdims=True)
    blend_ref[...] = jnp.broadcast_to(column / (snap[0].astype(jnp.float32) + 1.0), blend_ref.shape)

    def opp_copy(p, k, which):
        return remote(
            term.at[p, which, k], opp.at[which, k], opps.at[which, k], oppr.at[which, k],
            x_down if which == 0 else x_up,
        )

    def x_copy(p, k, side, part):
        return remote(
            term.at[p, part, k], xrecv.at[side, part, k], xs.at[side, part, k], xr.at[side, part, k],
            x_down if side == 0 else x_up,
        )

    def absorb(p, k, which):
        opp_copy(p, k, which).wait_recv()

        def body(i, carry):
            at = pl.ds(pl.multiple_of(i * 48, 16), 48)
            own = term[p, which, k, at, :].astype(jnp.float32)
            come = opp[which, k, at, :].astype(jnp.float32)
            term[p, which, k, at, :] = (own + come).astype(jnp.bfloat16)
            return carry

        lax.fori_loop(0, piece // 48, body, 0)
        x_copy(p, k, which, which).start()

    spans = []
    for k in range(NK):
        found = []
        for t in range(NH):
            for h in range(2):
                lo = max(t * third, h * token_block + k * piece)
                hi = min((t + 1) * third, h * token_block + (k + 1) * piece)
                if hi > lo:
                    found.append((t, lo, hi - lo))
        assert len({t for t, _, _ in found}) == len(found)
        spans.append(found)

    def h_copy(k, t, lo, size):
        return remote(
            zsum.at[pl.ds(lo, size)], zrecv.at[zh, pl.ds(lo - t * third, size)], hs.at[k, t], hr.at[k, zh],
            {"col": x * NH + t},
        )

    def h_arrival(k, source, lo, size):
        t = lo // third
        return remote(
            zsum.at[pl.ds(lo, size)], zrecv.at[source, pl.ds(lo - t * third, size)], hs.at[k, t],
            hr.at[k, source], {"col": x * NH + source},
        )

    def h_send(k):
        for kk in range(NK):

            @pl.when(k == kk)
            def _():
                for t, lo, size in spans[kk]:

                    @pl.when(zh != t)
                    def _():
                        h_copy(kk, t, lo, size).start()

    def collect(k, send):
        for part in range(2):
            for side in range(2):
                x_copy(x, k, side, part).wait_recv()

            def body(i, carry):
                at = pl.ds(pl.multiple_of(i * 48, 16), 48)
                total = (
                    term[x, part, k, at, :].astype(jnp.float32)
                    + xrecv[0, part, k, at, :].astype(jnp.float32)
                    + xrecv[1, part, k, at, :].astype(jnp.float32)
                )
                to = pl.ds(pl.multiple_of(part * token_block + k * piece + i * 48, 16), 48)
                zsum[to, :] = total.astype(jnp.bfloat16)
                return carry

            lax.fori_loop(0, piece // 48, body, 0)
        if send is True:
            h_send(k)
        else:

            @pl.when(send)
            def _():
                h_send(k)

    def events(s):
        return (look(below, s), look(above, s))

    def duty(s, send):
        for e in events(s - ABSORB):
            p, k = e // NK, e % NK

            @pl.when((e >= 0) & ((x + NZ - p) % NZ == 1))
            def _():
                absorb(p, k, 0)

            @pl.when((e >= 0) & ((x + NZ - p) % NZ == 3))
            def _():
                absorb(p, k, 1)

        for e in events(s - COLLECT):
            p, k = e // NK, e % NK

            @pl.when((e >= 0) & (p == x))
            def _():
                collect(k, send)

    def product(q, k):
        c_arrival(q, k).wait_recv()
        tokens = portion[q, k].reshape(2 * piece, hidden)
        part = lax.dot_general(
            tokens, wgt[...], (((1,), (1,)), ((), ())), preferred_element_type=jnp.float32
        )
        term[q, :, k] = (part * multiplier).astype(jnp.bfloat16).reshape(2, piece, wgt.shape[0])
        rel = (x + NZ - q) % NZ

        @pl.when(rel == 2)
        def _():
            opp_copy(q, k, 0).start()
            opp_copy(q, k, 1).start()

        @pl.when(rel == 1)
        def _():
            x_copy(q, k, 0, 1).start()

        @pl.when(rel == 3)
        def _():
            x_copy(q, k, 1, 0).start()

    def outer(q, k):
        both = pl.ds(k + 1 - NK // 2, NK // 2)
        tokens = portion[q, both].reshape(token_block, hidden)
        acc[...] += lax.dot_general(
            inp[q, both].reshape(token_block, acc.shape[0]), tokens, (((0,), (0,)), ((), ())),
            preferred_element_type=jnp.float32,
        )

    def deferred(s, carry):
        for e in events(s):

            @pl.when((e >= 0) & (e // NK == x))
            def _():
                h_send(e % NK)

        return carry

    def step(s, carry):
        hear(s + 1)
        pair = events(s)

        @pl.when(s >= NK)
        def _():
            for way, e, more in ((0, pair[0], more_up), (1, pair[1], more_down)):
                q, k = e // NK, e % NK
                onward = zl < NZ - 1 if way == 0 else zl > 0

                @pl.when(e >= 0)
                def _():
                    z_copy(way, q, k).wait_recv()

                    @pl.when(onward)
                    def _():
                        z_copy(way, q, k).start()

                    c_copy(q, k).start()
                    own = look(more, s)

                    @pl.when((own >= 0) & onward)
                    def _():
                        z_copy(way, zl, own).start()

        def products(j, carry):
            e = jnp.where(j == 0, pair[0], pair[1])

            @pl.when(e >= 0)
            def _():
                product(e // NK, e % NK)

            return carry

        def outers(j, carry):
            e = jnp.where(j == 0, pair[0], pair[1])

            @pl.when((e >= 0) & ((e + 1) % (NK // 2) == 0))
            def _():
                outer(e // NK, e % NK)

            return carry

        lax.fori_loop(0, 2, products, 0)
        duty(s, s < 0)
        lax.fori_loop(0, 2, outers, 0)
        return carry

    lax.fori_loop(0, last, step, 0)

    outside = (zl == 0) | (zl == NZ - 1)

    @pl.when(outside)
    def _():
        lax.fori_loop(0, last - COLLECT, deferred, 0)

    def y_copy(way, i):
        return remote(ysend.at[way, i], yrecv.at[way, i], ys.at[way, i], yr.at[way, i], y_peer[way])

    def y_step(i, carry):
        for way in range(2):
            k = groups // 2 - (i + 1) // 2
            target = (y + k) % groups if way == 0 else (y + groups - k) % groups
            which = (i + way) % 2
            rows = pl.ds(pl.multiple_of(target * shard, 8), shard)
            window = pl.ds(pl.multiple_of(which * cols, 128), cols)

            @pl.when(i < 2)
            def _():
                ysend[way, i] = acc[rows, window].astype(jnp.bfloat16)

            @pl.when(i >= 2)
            def _():
                y_copy(way, i - 2).wait_recv()
                ysend[way, i] = (acc[rows, window] + yrecv[way, i - 2].astype(jnp.float32)).astype(jnp.bfloat16)

            y_copy(way, i).start()

        go = jnp.int32(-1)
        for at, after in TAIL.items():
            go = jnp.where(i == at, after, go)

        @pl.when((i == HOLD) & jnp.logical_not(outside))
        def _():
            lax.fori_loop(0, last - COLLECT + sum(at < HOLD for at in TAIL), deferred, 0)

        @pl.when(go >= 0)
        def _():
            duty(last + go, outside | (i >= HOLD))

        return carry

    lax.fori_loop(0, STEPS, y_step, 0)

    rows = pl.ds(pl.multiple_of(y * shard, 16), shard)
    for way in range(2):
        for i in (STEPS - 2, STEPS - 1):
            y_copy(way, i).wait_recv()
    total_tokens = (NZ * 2 * token_block) * groups
    for window, up, down in (
        (slice(0, cols), STEPS - 1, STEPS - 2),
        (slice(cols, 2 * cols), STEPS - 2, STEPS - 1),
    ):
        share = acc[rows, window] + yrecv[0, up].astype(jnp.float32) + yrecv[1, down].astype(jnp.float32)
        step_ref[:, window] = wgt[rows, window].astype(jnp.float32) - learning_rate * (share / total_tokens**0.5)

    for t in range(NH):

        @pl.when(zh == t)
        def _():
            for source in range(NH):
                if source != t:
                    for k in range(NK):
                        for owner, lo, size in spans[k]:
                            if owner == t:
                                h_arrival(k, source, lo, size).wait_recv()
            others = [source for source in range(NH) if source != t]
            igrad_ref[...] = (
                zsum[pl.ds(t * third, third), :].astype(jnp.float32)
                + zrecv[others[0]].astype(jnp.float32)
                + zrecv[others[1]].astype(jnp.float32)
            ).astype(jnp.bfloat16)

    def drain(q, carry):
        for k in range(NK):
            c_copy(q, k).wait_send()

            @pl.when((q <= zl) & (zl < NZ - 1))
            def _():
                z_copy(0, q, k).wait_send()

            @pl.when((q >= zl) & (zl > 0))
            def _():
                z_copy(1, q, k).wait_send()

        return carry

    lax.fori_loop(0, NZ, drain, 0)
    for k in range(NK):
        for which in range(2):
            opp_copy((x + 2) % NZ, k, which).wait_send()
            x_copy((x + NZ - 1) % NZ, k, 0, which).wait_send()
            x_copy((x + 1) % NZ, k, 1, which).wait_send()
        for t, lo, size in spans[k]:

            @pl.when(zh != t)
            def _():
                h_copy(k, t, lo, size).wait_send()

    def y_drain(i, carry):
        y_copy(0, i).wait_send()
        y_copy(1, i).wait_send()
        return carry

    lax.fori_loop(0, STEPS, y_drain, 0)


def finish(step_ref, igrad_ref, blend_ref, mean_ref, square_ref, igrad_out, step_out, mean_out, square_out):
    igrad_out[...] = igrad_ref[...]
    blend = blend_ref[:, :1]
    stepped = step_ref[...]
    step_out[0] = stepped
    mean_old, square_old = mean_ref[0], square_ref[0]
    mean_out[0] = mean_old + blend * (stepped - mean_old)
    square_out[0] = square_old + blend * (stepped * stepped - square_old)


def body(inputs, pre_act, out_grad, weight, swag_mean, swag_square, snapshots, update_flag):
    tokens, width = inputs.shape
    block, hidden = pre_act.shape
    groups = lax.axis_size("dp")
    shard = width // groups
    piece = block // NK
    third = 2 * block // NH
    bf, f32 = jnp.bfloat16, jnp.float32
    dma = pltpu.SemaphoreType.DMA
    vmem = pl.BlockSpec(memory_space=pltpu.VMEM)
    stepped, igrad, blend = pl.pallas_call(
        kernel,
        out_shape=(
            jax.ShapeDtypeStruct((shard, hidden), f32),
            jax.ShapeDtypeStruct((third, width), bf),
            jax.ShapeDtypeStruct((shard, 128), f32),
        ),
        in_specs=[pl.BlockSpec(memory_space=pl.ANY)] * 6,
        out_specs=(vmem, vmem, vmem),
        scratch_shapes=[
            pltpu.SMEM((1,), jnp.int32),
            pltpu.VMEM((1, shard), jnp.int32),
            pltpu.VMEM((NZ, NK, 2, piece, width), bf),
            pltpu.VMEM((block, hidden), bf),
            pltpu.VMEM((block, hidden), bf),
            pltpu.VMEM((width, hidden), bf),
            pltpu.VMEM((NZ, NK, 2, piece, hidden), bf),
            pltpu.VMEM((width, hidden), f32),
            pltpu.VMEM((NZ, 2, NK, piece, width), bf),
            pltpu.VMEM((2, NK, piece, width), bf),
            pltpu.VMEM((2, 2, NK, piece, width), bf),
            pltpu.VMEM((2 * block, width), bf),
            pltpu.VMEM((NH, third, width), bf),
            pltpu.VMEM((2, STEPS, shard, hidden // 2), bf),
            pltpu.VMEM((2, STEPS, shard, hidden // 2), bf),
            dma((5 + 2 * NZ,)),
            dma((2, NZ, NK)), dma((NZ, NK)), dma((NZ, NK)), dma((NZ, NK)),
            dma((2, NK)), dma((2, NK)), dma((2, 2, NK)), dma((2, 2, NK)), dma((NK, NH)), dma((NK, NH)),
            dma((2, STEPS)), dma((2, STEPS)),
            pltpu.SemaphoreType.REGULAR((2,)),
        ],
        compiler_params=pltpu.CompilerParams(collective_id=0, has_side_effects=True),
    )(inputs.reshape(NZ, 2, NK, piece, width), pre_act, out_grad, weight, snapshots, update_flag)

    moments = jax.ShapeDtypeStruct(swag_mean.shape, f32)
    return pl.pallas_call(
        finish,
        out_shape=(jax.ShapeDtypeStruct(igrad.shape, bf), moments, moments, moments),
        in_specs=[vmem] * 5,
        out_specs=(vmem, vmem, vmem, vmem),
    )(stepped, igrad, blend, swag_mean, swag_square)


def solution(mesh):
    in_specs = (
        P("dp", "row"),
        P(("dp", "row"), "col"),
        P(("dp", "row"), "col"),
        P("row", "col"),
        P("dp", "row", "col"),
        P("dp", "row", "col"),
        P(),
        P("dp", "row"),
    )
    out_specs = (
        P(("dp", "col"), "row"),
        P("dp", "row", "col"),
        P("dp", "row", "col"),
        P("dp", "row", "col"),
    )
    return jax.shard_map(body, mesh=mesh, in_specs=in_specs, out_specs=out_specs, check_vma=False)
```

```python
import jax
import jax.numpy as jnp
from jax import lax
from jax.experimental import pallas as pl
from jax.experimental.pallas import tpu as pltpu
from jax.sharding import PartitionSpec as P

MESH = pl.DeviceIdType.MESH
D = 6144
learning_rate = 0.5
NZ = 4
NH = 3
NK = 2
STEPS = 7
ABSORB, COLLECT = 1, 3
HOLD = (3, 1, -1)
TAIL = {1: 0, 3: 1, 4: 2}
REACH = NZ * (NH - 1)
PER = 6


def gelu_slope(values):
    normal_cdf = 0.5 * (1.0 + lax.erf(values * 0.7071067811865476))
    density = jnp.exp(-0.5 * values * values) * 0.3989422804014327
    return normal_cdf + values * density


def remote(src, dst, send_sem, recv_sem, device):
    return pltpu.make_async_remote_copy(
        src_ref=src, dst_ref=dst, send_sem=send_sem, recv_sem=recv_sem, device_id=device, device_id_type=MESH
    )


def send_orders():
    orders, starts, extras = [], [], []
    arriving = []
    for z in range(NZ):
        own = [(z, k) for k in range(NK)]
        first = NK if z == 0 else min(NK, 2 if z == NZ - 2 else 1)
        start, rest = own[:first], own[first:]
        order, extra = list(start), []
        for piece in arriving:
            order.append(piece)
            if rest:
                extra.append(rest[0][1])
                order.append(rest.pop(0))
            else:
                extra.append(-1)
        order += rest
        orders.append(order)
        starts.append(first)
        extras.append(extra)
        arriving = order
    return orders, starts, extras


def packed(entries, length):
    words = []
    for line in entries:
        line = list(line) + [-1] * (length - len(line))
        line = [e + 1 for e in line]
        words.append([
            sum(e << (5 * i) for i, e in enumerate(line[w : w + PER])) for w in range(0, length, PER)
        ])
    return words


def choose(words, zl):
    out = []
    for w in range(len(words[0])):
        value = jnp.int32(words[0][w])
        for v in range(1, NZ):
            value = jnp.where(zl == v, jnp.int32(words[v][w]), value)
        out.append(value)
    return out


def look(words, s):
    value = jnp.int32(0)
    for w, word in enumerate(words):
        value = jnp.where((s >= PER * w) & (s < PER * (w + 1)), word, value)
    return ((value >> (5 * ((s + PER) % PER))) & 31) - 1


def kernel(
    inputs_hbm, pre_hbm, out_hbm, weight_hbm, snap_hbm, flag_hbm, step_ref, igrad_ref, blend_ref,
    snap, flag, inp, pre, outg, wgt, portion, acc, term, opp, xrecv, zsum, zrecv, ysend, yrecv,
    load_sem, zs, zr, cs, cr, opps, oppr, xs, xr, hs, hr, ys, yr, token,
):
    groups = lax.axis_size("dp")
    y = lax.axis_index("dp")
    row = lax.axis_index("row")
    col = lax.axis_index("col")
    zl, c = row // 2, row % 2
    x, zh = col // NH, col % NH
    multiplier = 1.0 / D**0.5
    token_block = pre.shape[0]
    piece = token_block // NK
    hidden = portion.shape[-1]
    shard = acc.shape[0] // groups
    cols = acc.shape[1] // 2
    third = 2 * token_block // NH
    last = NZ * NK

    partner = {"row": row + 1 - 2 * c}
    z_up, z_down = {"row": row + 2}, {"row": row - 2}
    x_up = {"col": (x + 1) % NZ * NH + zh}
    x_down = {"col": (x + NZ - 1) % NZ * NH + zh}
    y_peer = [{"dp": (y + 1) % groups}, {"dp": (y + groups - 1) % groups}]

    barrier = pltpu.get_barrier_semaphore()
    greet = [partner, x_up, x_down, *y_peer]
    for device in greet:
        pl.semaphore_signal(barrier, inc=1, device_id=device, device_id_type=MESH)
    chain = NZ * NH - 1
    place = zh * NZ + zl
    line_up = {"row": (row + 2) % (2 * NZ), "col": (col + (zl + 1) // NZ) % (NZ * NH)}
    line_down = {"row": (row + 2 * NZ - 2) % (2 * NZ), "col": (col + NZ * NH - (NZ - zl) // NZ) % (NZ * NH)}

    @pl.when(place < chain)
    def _():
        pl.semaphore_signal(barrier, inc=1, device_id=line_up, device_id_type=MESH)

    @pl.when(place > 0)
    def _():
        pl.semaphore_signal(barrier, inc=1, device_id=line_down, device_id_type=MESH)

    arrivals = len(greet) + jnp.minimum(place, 1) + jnp.minimum(chain - place, 1)

    def hear(n):
        for way, there, onward, device in (
            (0, place - n >= 0, place < chain, line_up), (1, place + n <= chain, place > 0, line_down),
        ):

            @pl.when((n >= 2) & (n <= REACH) & there)
            def _():
                pl.semaphore_wait(token.at[way], 1)

            @pl.when((n < REACH) & there & onward)
            def _():
                pl.semaphore_signal(token.at[way], inc=1, device_id=device, device_id_type=MESH)

    loads = [
        pltpu.make_async_copy(pre_hbm, pre, load_sem.at[0]),
        pltpu.make_async_copy(out_hbm, outg, load_sem.at[1]),
        pltpu.make_async_copy(weight_hbm, wgt, load_sem.at[2]),
        pltpu.make_async_copy(snap_hbm, snap, load_sem.at[3]),
        pltpu.make_async_copy(flag_hbm, flag, load_sem.at[4]),
        *(
            pltpu.make_async_copy(inputs_hbm.at[q, h], inp.at[q, :, h], load_sem.at[5 + 2 * q + h])
            for q in range(NZ)
            for h in range(2)
        ),
    ]
    for load in loads:
        load.start()

    orders, starts, extras = send_orders()
    code = lambda line: [q * NK + k for q, k in line]
    flip = lambda line: [(NZ - 1 - q, k) for q, k in line]
    own_steps = [[(z, k) for k in range(NK)] for z in range(NZ)]
    none = [-1] * NK
    below = [code(own_steps[z]) + (code(orders[z - 1]) if z > 0 else []) for z in range(NZ)]
    above = [none + (code(flip(orders[NZ - 2 - z])) if z < NZ - 1 else []) for z in range(NZ)]
    more_up = [none + extras[z] for z in range(NZ)]
    more_down = [none + extras[NZ - 1 - z] for z in range(NZ)]
    start_up = choose([[starts[z]] for z in range(NZ)], zl)[0]
    start_down = choose([[starts[NZ - 1 - z]] for z in range(NZ)], zl)[0]
    below, above, more_up, more_down = (
        choose(packed(t, last), zl) for t in (below, above, more_up, more_down)
    )

    def z_copy(way, q, k):
        block = portion.at[q, k, c]
        return remote(block, block, zs.at[way, q, k], zr.at[q, k], z_up if way == 0 else z_down)

    def c_copy(q, k):
        block = portion.at[q, k, c]
        return remote(block, block, cs.at[q, k], cr.at[q, k], partner)

    def c_arrival(q, k):
        block = portion.at[q, k, 1 - c]
        return remote(block, block, cs.at[q, k], cr.at[q, k], partner)

    tile = 16

    def local_grad(k):
        def body(i, carry):
            start = pl.multiple_of(i * tile, tile)
            a = pre[pl.ds(pl.multiple_of(k * piece + start, tile), tile), :].astype(jnp.float32)
            g = outg[pl.ds(pl.multiple_of(k * piece + start, tile), tile), :].astype(jnp.float32)
            portion[zl, k, c, pl.ds(start, tile), :] = (g * gelu_slope(a)).astype(jnp.bfloat16)
            return carry

        lax.fori_loop(0, piece // tile, body, 0)

    loads[0].wait()
    loads[1].wait()
    for k in range(NK):
        local_grad(k)
        if k == 0:
            pl.semaphore_wait(barrier, arrivals)

        @pl.when((zl < NZ - 1) & (k < start_up))
        def _():
            z_copy(0, zl, k).start()

        @pl.when((zl > 0) & (k < start_down))
        def _():
            z_copy(1, zl, k).start()

        c_copy(zl, k).start()

    def zero(i, carry):
        acc[pl.ds(pl.multiple_of(i * 8, 8), 8), :] = jnp.zeros((8, acc.shape[1]), jnp.float32)
        return carry

    lax.fori_loop(0, acc.shape[0] // 8, zero, 0)
    for load in loads[2:]:
        load.wait()
    flags = jnp.broadcast_to(flag[...].astype(jnp.float32), (shard, shard))
    here = lax.broadcasted_iota(jnp.int32, (shard, shard), 0) == lax.broadcasted_iota(jnp.int32, (shard, shard), 1)
    column = jnp.sum(jnp.where(here, flags, 0.0), axis=1, keepdims=True)
    blend_ref[...] = jnp.broadcast_to(column / (snap[0].astype(jnp.float32) + 1.0), blend_ref.shape)

    def opp_copy(p, k, which):
        return remote(
            term.at[p, which, k], opp.at[which, k], opps.at[which, k], oppr.at[which, k],
            x_down if which == 0 else x_up,
        )

    def x_copy(p, k, side, part):
        return remote(
            term.at[p, part, k], xrecv.at[side, part, k], xs.at[side, part, k], xr.at[side, part, k],
            x_down if side == 0 else x_up,
        )

    def absorb(p, k, which):
        opp_copy(p, k, which).wait_recv()

        def body(i, carry):
            at = pl.ds(pl.multiple_of(i * 48, 16), 48)
            own = term[p, which, k, at, :].astype(jnp.float32)
            come = opp[which, k, at, :].astype(jnp.float32)
            term[p, which, k, at, :] = (own + come).astype(jnp.bfloat16)
            return carry

        lax.fori_loop(0, piece // 48, body, 0)
        x_copy(p, k, which, which).start()

    spans = []
    for k in range(NK):
        found = []
        for t in range(NH):
            for h in range(2):
                lo = max(t * third, h * token_block + k * piece)
                hi = min((t + 1) * third, h * token_block + (k + 1) * piece)
                if hi > lo:
                    found.append((t, lo, hi - lo))
        assert len({t for t, _, _ in found}) == len(found)
        spans.append(found)

    def h_copy(k, t, lo, size):
        return remote(
            zsum.at[pl.ds(lo, size)], zrecv.at[zh, pl.ds(lo - t * third, size)], hs.at[k, t], hr.at[k, zh],
            {"col": x * NH + t},
        )

    def h_arrival(k, source, lo, size):
        t = lo // third
        return remote(
            zsum.at[pl.ds(lo, size)], zrecv.at[source, pl.ds(lo - t * third, size)], hs.at[k, t],
            hr.at[k, source], {"col": x * NH + source},
        )

    def h_send(k):
        for kk in range(NK):

            @pl.when(k == kk)
            def _():
                for t, lo, size in spans[kk]:

                    @pl.when(zh != t)
                    def _():
                        h_copy(kk, t, lo, size).start()

    def collect(k, send):
        for part in range(2):
            for side in range(2):
                x_copy(x, k, side, part).wait_recv()

            def body(i, carry):
                at = pl.ds(pl.multiple_of(i * 48, 16), 48)
                total = (
                    term[x, part, k, at, :].astype(jnp.float32)
                    + xrecv[0, part, k, at, :].astype(jnp.float32)
                    + xrecv[1, part, k, at, :].astype(jnp.float32)
                )
                to = pl.ds(pl.multiple_of(part * token_block + k * piece + i * 48, 16), 48)
                zsum[to, :] = total.astype(jnp.bfloat16)
                return carry

            lax.fori_loop(0, piece // 48, body, 0)
        if send is True:
            h_send(k)
        else:

            @pl.when(send)
            def _():
                h_send(k)

    def events(s):
        return (look(below, s), look(above, s))

    def duty(s, send):
        for e in events(s - ABSORB):
            p, k = e // NK, e % NK

            @pl.when((e >= 0) & ((x + NZ - p) % NZ == 1))
            def _():
                absorb(p, k, 0)

            @pl.when((e >= 0) & ((x + NZ - p) % NZ == 3))
            def _():
                absorb(p, k, 1)

        for e in events(s - COLLECT):
            p, k = e // NK, e % NK

            @pl.when((e >= 0) & (p == x))
            def _():
                collect(k, send)

    def product(q, k):
        c_arrival(q, k).wait_recv()
        tokens = portion[q, k].reshape(2 * piece, hidden)
        part = lax.dot_general(
            tokens, wgt[...], (((1,), (1,)), ((), ())), preferred_element_type=jnp.float32
        )
        term[q, :, k] = (part * multiplier).astype(jnp.bfloat16).reshape(2, piece, wgt.shape[0])
        rel = (x + NZ - q) % NZ

        @pl.when(rel == 2)
        def _():
            opp_copy(q, k, 0).start()
            opp_copy(q, k, 1).start()

        @pl.when(rel == 1)
        def _():
            x_copy(q, k, 0, 1).start()

        @pl.when(rel == 3)
        def _():
            x_copy(q, k, 1, 0).start()

    def outer(q, k):
        both = pl.ds(k + 1 - NK // 2, NK // 2)
        tokens = portion[q, both].reshape(token_block, hidden)
        acc[...] += lax.dot_general(
            inp[q, both].reshape(token_block, acc.shape[0]), tokens, (((0,), (0,)), ((), ())),
            preferred_element_type=jnp.float32,
        )

    def deferred(s, carry):
        for e in events(s):

            @pl.when((e >= 0) & (e // NK == x))
            def _():
                h_send(e % NK)

        return carry

    def step(s, carry):
        hear(s + 1)
        pair = events(s)

        @pl.when(s >= NK)
        def _():
            for way, e, more in ((0, pair[0], more_up), (1, pair[1], more_down)):
                q, k = e // NK, e % NK
                onward = zl < NZ - 1 if way == 0 else zl > 0

                @pl.when(e >= 0)
                def _():
                    z_copy(way, q, k).wait_recv()

                    @pl.when(onward)
                    def _():
                        z_copy(way, q, k).start()

                    c_copy(q, k).start()
                    own = look(more, s)

                    @pl.when((own >= 0) & onward)
                    def _():
                        z_copy(way, zl, own).start()

        def products(j, carry):
            e = jnp.where(j == 0, pair[0], pair[1])

            @pl.when(e >= 0)
            def _():
                product(e // NK, e % NK)

            return carry

        def outers(j, carry):
            e = jnp.where(j == 0, pair[0], pair[1])

            @pl.when((e >= 0) & ((e + 1) % (NK // 2) == 0))
            def _():
                outer(e // NK, e % NK)

            return carry

        lax.fori_loop(0, 2, products, 0)
        duty(s, s < 0)
        lax.fori_loop(0, 2, outers, 0)
        return carry

    lax.fori_loop(0, last, step, 0)

    hold = jnp.where(zh == 0, HOLD[0], jnp.where(zh == 1, HOLD[1], HOLD[2]))

    @pl.when(hold < 0)
    def _():
        lax.fori_loop(0, last - COLLECT, deferred, 0)

    def y_copy(way, i):
        return remote(ysend.at[way, i], yrecv.at[way, i], ys.at[way, i], yr.at[way, i], y_peer[way])

    def y_step(i, carry):
        for way in range(2):
            k = groups // 2 - (i + 1) // 2
            target = (y + k) % groups if way == 0 else (y + groups - k) % groups
            which = (i + way) % 2
            rows = pl.ds(pl.multiple_of(target * shard, 8), shard)
            window = pl.ds(pl.multiple_of(which * cols, 128), cols)

            @pl.when(i < 2)
            def _():
                ysend[way, i] = acc[rows, window].astype(jnp.bfloat16)

            @pl.when(i >= 2)
            def _():
                y_copy(way, i - 2).wait_recv()
                ysend[way, i] = (acc[rows, window] + yrecv[way, i - 2].astype(jnp.float32)).astype(jnp.bfloat16)

            y_copy(way, i).start()

        go = jnp.int32(-1)
        for at, after in TAIL.items():
            go = jnp.where(i == at, after, go)

        @pl.when(i == hold)
        def _():
            done = sum(jnp.where(at < hold, 1, 0) for at in TAIL)
            lax.fori_loop(0, last - COLLECT + done, deferred, 0)

        @pl.when(go >= 0)
        def _():
            duty(last + go, i >= hold)

        return carry

    lax.fori_loop(0, STEPS, y_step, 0)

    rows = pl.ds(pl.multiple_of(y * shard, 16), shard)
    for way in range(2):
        for i in (STEPS - 2, STEPS - 1):
            y_copy(way, i).wait_recv()
    total_tokens = (NZ * 2 * token_block) * groups
    for window, up, down in (
        (slice(0, cols), STEPS - 1, STEPS - 2),
        (slice(cols, 2 * cols), STEPS - 2, STEPS - 1),
    ):
        share = acc[rows, window] + yrecv[0, up].astype(jnp.float32) + yrecv[1, down].astype(jnp.float32)
        step_ref[:, window] = wgt[rows, window].astype(jnp.float32) - learning_rate * (share / total_tokens**0.5)

    for t in range(NH):

        @pl.when(zh == t)
        def _():
            for source in range(NH):
                if source != t:
                    for k in range(NK):
                        for owner, lo, size in spans[k]:
                            if owner == t:
                                h_arrival(k, source, lo, size).wait_recv()
            others = [source for source in range(NH) if source != t]
            igrad_ref[...] = (
                zsum[pl.ds(t * third, third), :].astype(jnp.float32)
                + zrecv[others[0]].astype(jnp.float32)
                + zrecv[others[1]].astype(jnp.float32)
            ).astype(jnp.bfloat16)

    def drain(q, carry):
        for k in range(NK):
            c_copy(q, k).wait_send()

            @pl.when((q <= zl) & (zl < NZ - 1))
            def _():
                z_copy(0, q, k).wait_send()

            @pl.when((q >= zl) & (zl > 0))
            def _():
                z_copy(1, q, k).wait_send()

        return carry

    lax.fori_loop(0, NZ, drain, 0)
    for k in range(NK):
        for which in range(2):
            opp_copy((x + 2) % NZ, k, which).wait_send()
            x_copy((x + NZ - 1) % NZ, k, 0, which).wait_send()
            x_copy((x + 1) % NZ, k, 1, which).wait_send()
        for t, lo, size in spans[k]:

            @pl.when(zh != t)
            def _():
                h_copy(k, t, lo, size).wait_send()

    def y_drain(i, carry):
        y_copy(0, i).wait_send()
        y_copy(1, i).wait_send()
        return carry

    lax.fori_loop(0, STEPS, y_drain, 0)


def finish(step_ref, igrad_ref, blend_ref, mean_ref, square_ref, igrad_out, step_out, mean_out, square_out):
    igrad_out[...] = igrad_ref[...]
    blend = blend_ref[:, :1]
    stepped = step_ref[...]
    step_out[0] = stepped
    mean_old, square_old = mean_ref[0], square_ref[0]
    mean_out[0] = mean_old + blend * (stepped - mean_old)
    square_out[0] = square_old + blend * (stepped * stepped - square_old)


def body(inputs, pre_act, out_grad, weight, swag_mean, swag_square, snapshots, update_flag):
    tokens, width = inputs.shape
    block, hidden = pre_act.shape
    groups = lax.axis_size("dp")
    shard = width // groups
    piece = block // NK
    third = 2 * block // NH
    bf, f32 = jnp.bfloat16, jnp.float32
    dma = pltpu.SemaphoreType.DMA
    vmem = pl.BlockSpec(memory_space=pltpu.VMEM)
    stepped, igrad, blend = pl.pallas_call(
        kernel,
        out_shape=(
            jax.ShapeDtypeStruct((shard, hidden), f32),
            jax.ShapeDtypeStruct((third, width), bf),
            jax.ShapeDtypeStruct((shard, 128), f32),
        ),
        in_specs=[pl.BlockSpec(memory_space=pl.ANY)] * 6,
        out_specs=(vmem, vmem, vmem),
        scratch_shapes=[
            pltpu.SMEM((1,), jnp.int32),
            pltpu.VMEM((1, shard), jnp.int32),
            pltpu.VMEM((NZ, NK, 2, piece, width), bf),
            pltpu.VMEM((block, hidden), bf),
            pltpu.VMEM((block, hidden), bf),
            pltpu.VMEM((width, hidden), bf),
            pltpu.VMEM((NZ, NK, 2, piece, hidden), bf),
            pltpu.VMEM((width, hidden), f32),
            pltpu.VMEM((NZ, 2, NK, piece, width), bf),
            pltpu.VMEM((2, NK, piece, width), bf),
            pltpu.VMEM((2, 2, NK, piece, width), bf),
            pltpu.VMEM((2 * block, width), bf),
            pltpu.VMEM((NH, third, width), bf),
            pltpu.VMEM((2, STEPS, shard, hidden // 2), bf),
            pltpu.VMEM((2, STEPS, shard, hidden // 2), bf),
            dma((5 + 2 * NZ,)),
            dma((2, NZ, NK)), dma((NZ, NK)), dma((NZ, NK)), dma((NZ, NK)),
            dma((2, NK)), dma((2, NK)), dma((2, 2, NK)), dma((2, 2, NK)), dma((NK, NH)), dma((NK, NH)),
            dma((2, STEPS)), dma((2, STEPS)),
            pltpu.SemaphoreType.REGULAR((2,)),
        ],
        compiler_params=pltpu.CompilerParams(collective_id=0, has_side_effects=True),
    )(inputs.reshape(NZ, 2, NK, piece, width), pre_act, out_grad, weight, snapshots, update_flag)

    moments = jax.ShapeDtypeStruct(swag_mean.shape, f32)
    return pl.pallas_call(
        finish,
        out_shape=(jax.ShapeDtypeStruct(igrad.shape, bf), moments, moments, moments),
        in_specs=[vmem] * 5,
        out_specs=(vmem, vmem, vmem, vmem),
    )(stepped, igrad, blend, swag_mean, swag_square)


def solution(mesh):
    in_specs = (
        P("dp", "row"),
        P(("dp", "row"), "col"),
        P(("dp", "row"), "col"),
        P("row", "col"),
        P("dp", "row", "col"),
        P("dp", "row", "col"),
        P(),
        P("dp", "row"),
    )
    out_specs = (
        P(("dp", "col"), "row"),
        P("dp", "row", "col"),
        P("dp", "row", "col"),
        P("dp", "row", "col"),
    )
    return jax.shard_map(body, mesh=mesh, in_specs=in_specs, out_specs=out_specs, check_vma=False)
```
